32 devices in a mesh: seg: 2 (over x), smp: 8 (over z, y), snp: 2 (over core).
Axes of the slice: x: 2, y: 2, z: 4, core: 2. Of those that a mesh axis runs over, the one named last changes fastest.
Arguments:
- dosage: bfloat16 [4096, 8192], P('smp', ('seg', 'snp')), parts along dimension 1, may hold values from -48 to 48, as said below
Outputs:
- band_corr: float32 [3, 16, 512, 512], P(None, ('seg', 'snp'), 'smp'), parts along dimension 1
The draws below stay inside these ranges and needn't reach their ends.
There are 2 independent parts, one for each index of `seg`. The reference program is written for one: setup_inputs(seed, part) draws one part's arguments, and reference() takes and returns one part's arrays. A program takes and returns all parts, laid end to end along the dimension named above; each array names one. Nothing has to cross between parts.
Inputs may be any that keep to these rules, and one draw needn't show every extreme that they name: `dosage`: dosages of each SNP share part of their variation with SNPs nearby.
All inputs are finite; a program needn't handle non-finite values.
Results may differ from the reference program's by a relative error of at most 0.0003.
Values may be sent and summed in bfloat16 or wider, within the bound.
No kernel may reach another device: no remote copies, remote signals or barrier semaphores. Data moves between devices by JAX's collectives and lax.ppermute only.
A program may use at most 128 MiB of HBM per device.

```python
import jax
import jax.numpy as jnp
from jax import lax

BLK = 512
NBLK = 8
SNPS = 4096
SAMPLES = 4096


def draw_dosage(key, part):
    key_noise, key_factor, key_load, key_scale = jax.random.split(key, 4)
    factor_count = SNPS // 64
    noise = jax.random.normal(key_noise, (SAMPLES, SNPS), jnp.float32)
    col_scale = jax.random.uniform(key_scale, (SNPS,), jnp.float32, 0.5, 2.0)
    factors = jax.random.normal(key_factor, (SAMPLES, factor_count), jnp.float32)
    columns = jnp.arange(SNPS, dtype=jnp.float32)
    centers = 64.0 * jnp.arange(factor_count, dtype=jnp.float32) + 32.0
    nearby = (jnp.abs(columns[None, :] - centers[:, None]) < 640.0).astype(jnp.float32)
    loading = jax.random.uniform(key_load, (factor_count, SNPS), jnp.float32, -0.6, 0.6) * nearby
    mixed = noise + jnp.dot(factors, loading, precision=lax.Precision.HIGHEST)
    row_scale = 0.6 + 1.2 * jnp.arange(SAMPLES, dtype=jnp.float32) / SAMPLES
    return jnp.clip(mixed * row_scale[:, None] * col_scale[None, :], -48.0, 48.0).astype(jnp.bfloat16)


def setup_inputs(seed: int = 0, part: int = 0) -> dict:
    arg_keys = jax.random.split(jax.random.key(seed), 2)
    own_keys = jax.random.split(jax.random.fold_in(arg_keys[1], part), 2)
    dosage = draw_dosage(jax.random.fold_in(jax.random.fold_in(arg_keys[1], part), 71), part)
    return {"dosage": dosage}


epsilon = 1e-06

def reference(dosage):
    squares = lax.optimization_barrier(jnp.sum(jnp.square(dosage.astype(jnp.float32)), axis=0))
    padded = jnp.pad(dosage, ((0, 0), (0, 2 * BLK)))
    squares_pad = jnp.pad(squares, (0, 2 * BLK))

    def one_block(block):
        begin = (block * BLK).astype(jnp.int32)
        left_part = lax.dynamic_slice_in_dim(dosage, begin, BLK, 1).astype(jnp.float32)
        right_part = lax.dynamic_slice_in_dim(padded, begin, 3 * BLK, 1).astype(jnp.float32)
        gram = jnp.dot(left_part.T, right_part, precision=lax.Precision.HIGHEST, preferred_element_type=jnp.float32)
        row_scale = lax.rsqrt(lax.dynamic_slice_in_dim(squares, begin, BLK, 0) + epsilon)
        col_scale = lax.rsqrt(lax.dynamic_slice_in_dim(squares_pad, begin, 3 * BLK, 0) + epsilon)
        scaled = gram * row_scale[:, None] * col_scale[None, :]
        return scaled.reshape(BLK, 3, BLK).transpose(1, 0, 2)
    stacked = lax.map(one_block, jnp.arange(NBLK, dtype=jnp.int32))
    return stacked.transpose(1, 0, 2, 3)
```

```python
import functools

import jax
import jax.numpy as jnp
from jax import lax
from jax.experimental import pallas as pl
from jax.experimental.pallas import tpu as pltpu
from jax.sharding import PartitionSpec as P

BLK = 512
EPS = 1e-06
TINY = 1e-30
F32 = jnp.float32
F16 = jnp.float16


def mm(lt, right):
    return jnp.dot(lt, right, preferred_element_type=F32)


def tile_kernel(lefts, rights, pairs, where_ref, *refs):
    n_in = 2 * lefts
    ins, out, bufs, lt_ref, sems = refs[: n_in], refs[n_in], refs[n_in + 1], refs[n_in + 2], refs[n_in + 3]
    del rights
    odd, half = where_ref[0], where_ref[1]
    copies = []
    for j in range(lefts):
        for h in range(2):
            ref = ins[2 * j + h]
            if ref.shape[1] != BLK:
                begin = pl.multiple_of(where_ref[2 + j], BLK)
                ref = ref.at[:, pl.ds(begin, BLK)]
            copies.append(pltpu.make_async_copy(ref, bufs.at[j, h], sems.at[j, h]))
    for c in copies:
        c.start()
    for c in copies:
        c.wait()
    _, _, parts, _, tr, _ = lt_ref.shape

    def rows(j, h):
        lt_ref[j, h] = bufs[j, h].T.reshape(lt_ref.shape[2:])
        return lt_ref[j, h, :, half].reshape(parts * tr, -1)

    def emit(which):
        left_of = {}
        for m, (a, b) in enumerate(pairs[which]):
            if a not in left_of:
                left_of = {a: (rows(a, 0), rows(a, 1))}
            lo, lr = left_of[a]
            acc = mm(lo, bufs[b, 0]) + mm(lr, bufs[b, 1])
            out[:, m] = acc.reshape(parts, tr, BLK)

    if pairs[0] == pairs[1]:
        emit(0)
    else:
        pl.when(odd == 0)(functools.partial(emit, 0))
        pl.when(odd != 0)(functools.partial(emit, 1))


def tiles_of(where, blocks, pairs, n):
    samples = blocks[0][1].shape[0]
    tr = BLK // n
    count = len(pairs[0])
    k = len(blocks)
    flat = [x for pair in blocks for x in pair]
    return pl.pallas_call(
        functools.partial(tile_kernel, k, k, pairs),
        out_shape=jax.ShapeDtypeStruct((n // 2, count, tr, BLK), F32),
        in_specs=[pl.BlockSpec(memory_space=pltpu.SMEM)] + [pl.BlockSpec(memory_space=pl.ANY)] * (2 * k),
        out_specs=pl.BlockSpec(memory_space=pltpu.VMEM),
        scratch_shapes=[
            pltpu.VMEM((k, 2, samples, BLK), jnp.bfloat16),
            pltpu.VMEM((k, 2, n // 2, 2, tr, samples), jnp.bfloat16),
            pltpu.SemaphoreType.DMA((k, 2)),
        ],
        cost_estimate=pl.CostEstimate(
            flops=count * BLK * BLK * samples * 2, bytes_accessed=4 * k * samples * BLK + 2 * count * BLK * BLK, transcendentals=0
        ),
    )(where, *flat)


def shards(n, cores, dosage):
    samples, width = dosage.shape
    nb = width // BLK
    tr = BLK // n
    me = lax.axis_index("smp")
    core = lax.axis_index("snp")
    odd = core % 2
    bits = [1 << b for b in range(1, n.bit_length() - 1)]

    def swap(x, bit, only=None):
        if only is None:
            return lax.ppermute(x, "smp", [(i, i ^ bit) for i in range(n)])
        return lax.ppermute(x, ("smp", "snp"), [(i * cores + c, (i ^ bit) * cores + c) for i in range(n) for c in only])

    def from_next(x):
        return lax.ppermute(x, "snp", [(c + 1, c) for c in range(cores - 1)])

    def order(t):
        return jnp.where(odd == 0, nb - 1 - t, t)

    own = [lax.dynamic_slice_in_dim(dosage, order(t) * BLK, BLK, 1) for t in range(nb)]
    squares = jnp.sum(jnp.square(dosage.astype(F32)), axis=0)
    halo_own = from_next(dosage[:, : 2 * BLK])
    other = [swap(own[0], 1)]
    for bit in bits:
        squares = squares + swap(squares, bit)
    squares = squares + swap(squares, 1)
    for t in range(1, nb):
        other.append(swap(own[t], 1))
    halo_other = [from_next(other[0]), from_next(other[1])]
    halo_squares = from_next(squares[: 2 * BLK])
    square_sums = jnp.concatenate([squares, halo_squares]).reshape(nb + 2, BLK)
    send_scale = lax.rsqrt(jnp.maximum(square_sums, TINY))
    last_scale = lax.rsqrt(square_sums + EPS) / send_scale

    def row_part(scale):
        cube = scale.reshape(nb + 2, n, tr)
        return cube

    send_rows = send_scale.reshape(nb + 2, n // 2, 2, tr)
    send_rows = lax.dynamic_index_in_dim(send_rows, me % 2, 2, keepdims=False)
    last_rows = lax.dynamic_index_in_dim(last_scale.reshape(nb + 2, n, tr), me, 1, keepdims=False)

    where_base = [odd, me % 2]
    out = jnp.zeros((3, nb, tr, BLK), F32)

    def reduce(part, left_ids, right_ids, only=None):
        rs = jnp.stack([lax.dynamic_index_in_dim(send_rows, i, 0, keepdims=False) for i in left_ids], 1)
        cs = jnp.stack([lax.dynamic_index_in_dim(send_scale, i, 0, keepdims=False) for i in right_ids], 0)
        part = part * rs[..., None] * cs[None, :, None, :]
        for bit in bits:
            part = part.reshape((part.shape[0] // 2, 2) + part.shape[1:])
            mine = (me // bit) % 2
            sent = lax.dynamic_index_in_dim(part, 1 - mine, 1, keepdims=False).astype(F16)
            kept = lax.dynamic_index_in_dim(part, mine, 1, keepdims=False)
            part = kept + swap(sent, bit, only).astype(F32)
        part = part[0]
        lr = jnp.stack([lax.dynamic_index_in_dim(last_rows, i, 0, keepdims=False) for i in left_ids], 0)
        lc = jnp.stack([lax.dynamic_index_in_dim(last_scale, i, 0, keepdims=False) for i in right_ids], 0)
        return part * lr[:, :, None] * lc[:, None, :]

    def chunk(t):
        k = min(t, 2) + 1
        blocks = [(dosage, other[t - j]) for j in range(k)]
        where = jnp.stack(where_base + [order(t - j) * BLK for j in range(k)]).astype(jnp.int32)
        pairs = ([(0, j) for j in range(k)], [(j, 0) for j in range(k)])
        part = tiles_of(where, blocks, pairs, n)
        left = [jnp.where(odd == 0, order(t), order(t - j)) for j in range(k)]
        right = [jnp.where(odd == 0, order(t - j), order(t)) for j in range(k)]
        return reduce(part, left, right), left

    def halo_chunk():
        blocks = [(dosage, other[0]), (dosage, other[1]), (halo_own[:, :BLK], halo_other[0]), (halo_own[:, BLK:], halo_other[1])]
        where = jnp.stack(where_base + [(nb - 1) * BLK, (nb - 2) * BLK]).astype(jnp.int32)
        pairs = [(0, 2), (0, 3), (1, 2)]
        part = tiles_of(where, blocks, (pairs, pairs), n)
        last = core == cores - 1
        part = jnp.where(last, 0.0, part)
        return reduce(part, [nb - 1, nb - 1, nb - 2], [nb, nb + 1, nb], only=range(cores - 1))

    def place(out, tile, k, b):
        return lax.dynamic_update_slice(out, tile[None, None], (k, b, 0, 0))

    for t in range(nb):
        got, left = chunk(t)
        for m in range(got.shape[0]):
            out = place(out, got[m], m, left[m])
        if t == 1:
            halo = halo_chunk()
            for m, (k, b) in enumerate([(1, nb - 1), (2, nb - 1), (2, nb - 2)]):
                out = place(out, halo[m], k, b)
    return out


def solution(mesh):
    return jax.shard_map(
        functools.partial(shards, mesh.shape["smp"], mesh.shape["snp"]),
        mesh=mesh,
        in_specs=(P("smp", ("seg", "snp")),),
        out_specs=P(None, ("seg", "snp"), "smp", None),
        check_vma=False,
    )
```

```python
import functools

import jax
import jax.numpy as jnp
from jax import lax
from jax.experimental import pallas as pl
from jax.experimental.pallas import tpu as pltpu
from jax.sharding import PartitionSpec as P


BLK = 512
LANES = 128
EPS = 1e-06
BOOST = 2.0**15
F32 = jnp.float32
F16 = jnp.float16
BF16 = jnp.bfloat16
VM = pl.BlockSpec(memory_space=pltpu.VMEM)
PARAMS = pltpu.CompilerParams(vmem_limit_bytes=16 * 2**20)
ANY = pl.BlockSpec(memory_space=pl.ANY)


def mm(lt, right):
    return jnp.dot(lt, right, preferred_element_type=F32)


def vm(x):
    return pltpu.with_memory_space_constraint(x, pltpu.VMEM)


def odd_core():
    return lax.rem(lax.axis_index("snp"), 2)


def block_at(nb, t):
    return jnp.where(odd_core() == 0, nb - 1 - t, t)


def prep_kernel(nb, d_ref, *refs):
    outs, sq_ref, sems = refs[:nb], refs[nb], refs[nb + 1]
    copies = []
    for t in range(nb):
        begin = pl.multiple_of(block_at(nb, t) * BLK, BLK)
        copies.append(pltpu.make_async_copy(d_ref.at[:, pl.ds(begin, BLK)], outs[t], sems.at[t]))
        copies[t].start()
    for t in range(nb):
        copies[t].wait()
        f = outs[t][...].astype(F32)
        sq_ref[t : t + 1, :] = jnp.sum(f * f, axis=0, keepdims=True)


def put_rows(x, wide, dst, flip=0):
    me = lax.axis_index("smp")
    z, half = me // 2, lax.rem(me, 2) ^ flip
    wide[...] = x.T.reshape(wide.shape)
    for rel in range(wide.shape[0]):
        dst[rel] = wide[z ^ rel, half]


def rows_kernel(nb, *refs):
    ins, out, wide = refs[:nb], refs[nb], refs[nb + 1]
    for t in range(nb):
        put_rows(ins[t][...], wide.at[t], out.at[t])


def scale_kernel(a_ref, b_ref, col_ref, first_ref, rows_ref, flip_ref, wide):
    scale = lax.rsqrt(a_ref[...] + b_ref[...] + EPS)
    col_ref[...] = scale
    first_ref[...] = scale[:2]
    for t in range(a_ref.shape[0]):
        put_rows(jnp.broadcast_to(scale[t : t + 1] * BOOST, (LANES, BLK)), wide.at[t], rows_ref.at[t])
    put_rows(jnp.broadcast_to(scale[t : t + 1] * BOOST, (LANES, BLK)), wide.at[t], flip_ref, 1)


def emit(keep, send, m, acc, row, col):
    count, _, tr, _ = keep.shape
    acc = acc * col
    for i in range(BLK // LANES):
        part = (acc[:, i * LANES : (i + 1) * LANES] * row).reshape(count, 2, tr, LANES)
        keep[:, m, :, i * LANES : (i + 1) * LANES] = part[:, 0]
        send[:, m, :, i * LANES : (i + 1) * LANES] = part[:, 1]


def flat(x):
    return x.reshape(x.shape[0] * x.shape[1], x.shape[2])


def chunk_kernel(t, ms, new, cols, rows_ref, lown_ref, *refs):
    k = max(ms) + 1
    own, other = refs[:k], refs[k : 2 * k]
    if new:
        lother = refs[2 * k : 3 * k - 1]
        keep, send, lnew, wide = refs[3 * k - 1 :]
        put_rows(other[0][...], wide, lnew)
        lother = (lnew,) + tuple(lother)
    else:
        lother = refs[2 * k : 3 * k]
        keep, send = refs[3 * k :]

    def even():
        lo, lr = flat(lown_ref[t]), flat(lother[0][...])
        row = flat(rows_ref[t])
        for i, m in enumerate(ms):
            acc = mm(lo, own[m][...]) + mm(lr, other[m][...])
            emit(keep, send, i, acc, row, cols[t - m : t - m + 1, :])

    def uneven():
        ro, rr = own[0][...], other[0][...]
        col = cols[t : t + 1, :]
        for i, m in enumerate(ms):
            acc = mm(flat(lown_ref[t - m]), ro) + mm(flat(lother[m][...]), rr)
            emit(keep, send, i, acc, flat(rows_ref[t - m]), col)

    pl.when(odd_core() == 0)(even)
    pl.when(odd_core() != 0)(uneven)


def own_kernel(cols, rows_ref, flip_ref, lown_ref, own, keep, send, flipped, wide):
    t = cols.shape[0] - 1
    put_rows(own[...], wide, flipped, 1)
    for i, (lt, row) in enumerate(((lown_ref[t], rows_ref[t]), (flipped[...], flip_ref[...]))):
        emit(keep, send, i, mm(flat(lt), own[...]), flat(row), cols[t : t + 1, :])


HALO = ((1, 0, 0), (2, 0, 1), (2, 1, 0))


def halo_kernel(cores, cols, rows_ref, lown_ref, l0, l1, o0, o1, r0, r1, keep, send):
    last = lax.axis_index("snp") == cores - 1

    @pl.when(jnp.logical_not(last))
    def _():
        for m, (_, a, b) in enumerate(HALO):
            acc = mm(flat(lown_ref[a]), (o0, o1)[b][...]) + mm(flat((l0, l1)[a][...]), (r0, r1)[b][...])
            emit(keep, send, m, acc, flat(rows_ref[a]), cols[b : b + 1, :])

    @pl.when(last)
    def _():
        keep[...] = jnp.zeros_like(keep)
        send[...] = jnp.zeros_like(send)


def place_kernel(nb, names, *refs):
    tiles, out, sems = refs[: len(names)], refs[-2], refs[-1]
    copies = []
    for name, tile in zip(names, tiles):
        for i in range(tile.shape[0]):
            if name == "h":
                dst = out.at[HALO[i][0], nb - 1 - HALO[i][1]]
            else:
                t, m = name[0], name[1][i]
                dst = out.at[m, jnp.where(odd_core() == 0, nb - 1 - t, t - m)]
            copies.append(pltpu.make_async_copy(tile.at[i], dst, sems.at[len(copies)]))
    for c in copies:
        c.start()
    for c in copies:
        c.wait()


def kernel_call(body, out_shape, args, scratch=()):
    vmem_out = [pltpu.VMEM(s, t) for s, t in out_shape]
    return pl.pallas_call(
        body,
        out_shape=vmem_out,
        in_specs=[VM] * len(args),
        out_specs=[VM] * len(vmem_out),
        scratch_shapes=list(scratch),
        compiler_params=PARAMS,
    )(*[vm(a) for a in args])


def shards(n, cores, dosage):
    samples, width = dosage.shape
    nb = width // BLK
    tr = BLK // n
    zs = n // 2
    bits = [1 << b for b in range(1, n.bit_length() - 1)]

    def swap(x, bit, only=None):
        if only is None:
            return lax.ppermute(x, "smp", [(i, i ^ bit) for i in range(n)])
        return lax.ppermute(x, ("smp", "snp"), [(i * cores + c, (i ^ bit) * cores + c) for i in range(n) for c in only])

    def from_next(x):
        return lax.ppermute(x, "snp", [(c + 1, c) for c in range(cores - 1)])

    *own, squares = pl.pallas_call(
        functools.partial(prep_kernel, nb),
        out_shape=[pltpu.VMEM((samples, BLK), BF16)] * nb + [pltpu.VMEM((nb, BLK), F32)],
        in_specs=[ANY],
        out_specs=[VM] * (nb + 1),
        scratch_shapes=[pltpu.SemaphoreType.DMA((nb,))],
        compiler_params=PARAMS,
    )(dosage)
    got = swap(squares, 1)
    other = [swap(own[t], 1) for t in range(nb)]
    halo_own = [from_next(own[t]) for t in range(2)]
    lown = kernel_call(functools.partial(rows_kernel, nb), [((nb, zs, tr, samples), BF16)], own, [pltpu.VMEM((nb, zs, 2, tr, samples), BF16)])[0]
    for bit in bits:
        squares = squares + got
        got = swap(squares, bit)
    cols, first, rows, flip = kernel_call(
        scale_kernel,
        [((nb, BLK), F32), ((2, BLK), F32), ((nb, zs, tr, LANES), F32), ((zs, tr, LANES), F32)],
        [squares, got],
        [pltpu.VMEM((nb, zs, 2, tr, LANES), F32)],
    )
    halo_cols = from_next(first)

    def reduce(name, keep, send, only=None):
        terms = [keep, swap(send.astype(F16), bits[0], only)]
        for bit in bits[1:]:
            sent = sum(x[1::2].astype(F32) for x in terms).astype(F16)
            terms = [x[0::2] for x in terms] + [swap(sent, bit, only)]
        if name == "e":
            sent = sum(x[0, 1:].astype(F32) for x in terms).astype(F16)
            terms = [x[:, :1] for x in terms] + [swap(sent, 1)[None]]
        return sum(x[0].astype(F32) for x in terms) * (1.0 / BOOST)

    def place(out, tiles, names):
        count = sum(t.shape[0] for t in tiles)
        extra = [] if out is None else [out]
        return pl.pallas_call(
            functools.partial(place_kernel, nb, names),
            out_shape=jax.ShapeDtypeStruct((3, nb, tr, BLK), F32),
            in_specs=[VM] * len(tiles) + [ANY] * len(extra),
            out_specs=ANY,
            scratch_shapes=[pltpu.SemaphoreType.DMA((count,))],
            compiler_params=PARAMS,
            input_output_aliases={len(tiles): 0} if extra else {},
        )(*[vm(t) for t in tiles], *extra)

    lother = []
    keep, send, _ = kernel_call(
        own_kernel,
        [((zs // 2, 2, tr, BLK), F32)] * 2 + [((zs, tr, samples), BF16)],
        [cols, rows, flip, lown, own[nb - 1]],
        [pltpu.VMEM((zs, 2, tr, samples), BF16)],
    )
    parts = {(nb - 1, (0,)): ("e", keep, send)}
    for t in range(nb):
        for g, ms in enumerate(groups_of(t)):
            k = max(ms) + 1
            keep, send, *lnew = kernel_call(
                functools.partial(chunk_kernel, t, ms, g == 0),
                [((zs // 2, len(ms), tr, BLK), F32)] * 2 + [((zs, tr, samples), BF16)] * (g == 0),
                [cols, rows, lown] + [own[t - j] for j in range(k)] + [other[t - j] for j in range(k)] + [lother[t - j] for j in range(g == 0, k)],
                [pltpu.VMEM((zs, 2, tr, samples), BF16)] * (g == 0),
            )
            lother += lnew
            parts[t, ms] = (f"c{t}{g}", keep, send)
        if t == 1:
            halo_other = [from_next(other[j]) for j in range(2)]
            keep, send = kernel_call(
                functools.partial(halo_kernel, cores),
                [((zs // 2, len(HALO), tr, BLK), F32)] * 2,
                [halo_cols, rows, lown, lother[0], lother[1], *halo_own, *halo_other],
            )
            parts["h"] = ("h", keep, send, range(cores - 1))
    tiles = {key: reduce(*part) for key, part in parts.items()}
    final = (nb - 1, groups_of(nb - 1)[-1])
    early = [key for key in tiles if key != final]
    out = place(None, [tiles[key] for key in early], early)
    return place(out, [tiles[final]], [final])


def groups_of(t):
    return (((0,),), ((0, 1),), ((0, 1), (2,)), ((1,), (2,)))[t]


def solution(mesh):
    n, cores = mesh.shape["smp"], mesh.shape["snp"]

    def body(dosage):
        return shards(n, cores, dosage)

    return jax.shard_map(
        body,
        mesh=mesh,
        in_specs=(P("smp", ("seg", "snp")),),
        out_specs=P(None, ("seg", "snp"), "smp", None),
        check_vma=False,
    )
```
